32 devices in a mesh: dp: 4 (over x, core), expert: 8 (over z, y).
Axes of the slice: x: 2, y: 2, z: 4, core: 2. Of those that a mesh axis runs over, the one named last changes fastest.
Arguments:
- tokens: bfloat16 [4096, 1024], P(('dp', 'expert')), may hold values from -6 to 6
- expert_ids: int32 [4096, 1], P(('dp', 'expert')), may hold values from 0 to 7; in each aligned block of 128 rows (0 to 127, 128 to 255, ...) at most 48 rows name the same one
- gate_scale: float32 [4096], P(('dp', 'expert')), may hold values from 0.1 to 1
- w_gate_up: bfloat16 [8, 1024, 768], P('expert'), may hold values from -0.1875 to 0.1875
- w_down: bfloat16 [8, 1024, 384], P('expert'), may hold values from -0.3125 to 0.3125
- out_grad: bfloat16 [4096, 1024], P(('dp', 'expert')), may hold values from -1.5 to 1.5
Outputs:
- mixed: bfloat16 [4096, 1024], P(('dp', 'expert'))
- input_rows: bfloat16 [4096, 1024], P(('dp', 'expert'))
- gate_grad_rows: float32 [4096], P(('dp', 'expert'))
- grad_gate_up: float32 [8, 1024, 768], P('expert', 'dp')
- grad_down: float32 [8, 1024, 384], P('expert', 'dp')
The draws below stay inside these ranges and needn't reach their ends.
Inputs may be any that keep to these rules, and one draw needn't show every extreme that they name: `expert_ids`: among the rows of one device no expert is named more than 48 times, a bound that some block reaches.
All inputs are finite; a program needn't handle non-finite values.
Results may differ from the reference program's by a relative error of at most 0.017.
Values may be sent and summed in bfloat16 or wider, within the bound.
A program may use at most 64 MiB of HBM per device.

```python
import math
import jax
import jax.numpy as jnp
import numpy as np
from jax import lax

D = 1024
H = 384
ROWS_DEV = 128
BLOCK = 128
EXPERTS = 8
CAP = 48
TOKENS = 4096
N_DP = 4
N_EXPERT = 8


def shard_levels(key, shape, shards, least, high):
    def one(position, shards_of):
        draws = jax.random.uniform(jax.random.fold_in(jax.random.fold_in(key, 6), position), (shards_of,), jnp.float32, least / len(shards), high / len(shards))
        return jnp.repeat(jnp.exp(draws), shape[position] // shards_of).reshape((-1,) + (1,) * (len(shape) - position - 1))

    gain = one(*shards[0])
    for cut in shards[1:]:
        gain = gain * one(*cut)
    return gain


def deal_out(own_key, own, number, rows, amount, top, most, skew):
    sequence = jax.random.permutation(own_key, amount)
    packed, common = load_shares(amount, rows * top, most, skew, True), load_shares(amount, rows * top, most, skew, False)
    places = jnp.arange(amount)

    def named(tallies, turn):
        used = int((tallies > 0).sum())
        fixed = max(1, used // 4)
        passed = fixed + (places - fixed + turn * (used - fixed)) % max(1, amount - fixed)
        return jnp.zeros((amount,), jnp.int32).at[sequence[jnp.where(places < fixed, places, passed)]].set(jnp.asarray(tallies, jnp.int32))

    tallies = jnp.where(number % 4 == 0, named(packed, number // 4), named(common, number - number // 4 - 1))
    mixed = jax.random.permutation(jax.random.fold_in(own, 3), amount)
    giver, taker = mixed[0:amount // 2 * 2:2], mixed[1:amount // 2 * 2:2]
    margin = jnp.minimum(tallies[giver] - 1, most - tallies[taker]) // 2
    margin = jnp.where((giver == sequence[0]) | (taker == sequence[0]) | (tallies[taker] == 0), 0, jnp.maximum(margin, 0))
    passed = jax.random.randint(jax.random.fold_in(own, 4), (amount // 2,), 0, 1 << 20) % (margin + 1)
    tallies = tallies.at[giver].add(-passed).at[taker].add(passed)
    items = jnp.searchsorted(jnp.cumsum(tallies), jnp.arange(rows * top), side="right").astype(jnp.int32)
    table = items.reshape(top, rows).T
    table = table[jax.random.permutation(jax.random.fold_in(own, 1), rows)]
    turn = jax.random.randint(jax.random.fold_in(own, 2), (rows, 1), 0, top)
    return jnp.take_along_axis(table, (jnp.arange(top)[None, :] + turn) % top, axis=1)


def load_shares(amount, total, reach, lean, full):
    weights = [(1 << 20) // math.isqrt(grade ** lean) + 1 for grade in range(1, amount + 1)]
    largest = reach if full else min(reach, max(-(-total // amount), total * weights[0] // sum(weights)))
    least = 1 if total - largest >= amount - 1 else 0
    given, rest = [largest] + [least] * (amount - 1), total - largest - least * (amount - 1)
    while rest > 0:
        free = [i for i in range(1, amount) if given[i] < largest] or [i for i in range(1, amount) if given[i] < reach]
        mass, remaining = sum([weights[i] for i in free]), rest
        for i in free:
            extra = min(reach - given[i], max(1, remaining * weights[i] // mass), rest)
            given[i] = given[i] + extra
            rest = rest - extra
    return np.array(given)


def normal_values(key, shape, spread, limit, split=(), held_as=jnp.bfloat16):
    gain = shard_levels(key, shape, split, -0.22, 0.18) if split else 1.0
    array = jax.random.normal(key, shape, jnp.float32) * spread * gain
    return jnp.minimum(jnp.maximum(array, -limit), limit).astype(held_as)


def setup_inputs(seed: int = 0) -> dict:
    keys = jax.random.split(jax.random.key(seed), 7)
    tokens = normal_values(keys[0], (TOKENS, D), 1.0, 6.0, ((0, 32),))
    expert_ids_keys = jax.random.split(jax.random.fold_in(keys[1], 1), TOKENS // ROWS_DEV)
    expert_ids_turns = jax.random.permutation(jax.random.fold_in(keys[1], 3), TOKENS // ROWS_DEV)
    expert_ids = jax.vmap(lambda own, number: deal_out(jax.random.fold_in(keys[1], 2), own, number, ROWS_DEV, EXPERTS, 1, CAP, 2))(expert_ids_keys, expert_ids_turns).reshape((TOKENS, 1))
    gate_scale = jnp.clip(0.1 + 0.9 * jax.random.uniform(keys[2], (TOKENS,), jnp.float32) ** shard_levels(keys[2], (TOKENS,), ((0, 32),), -0.2, 0.2), 0.1, 1.0)
    w_gate_up = normal_values(keys[3], (EXPERTS, D, 2 * H), D ** -0.5, 0.1875, ((0, 8),))
    w_down = normal_values(keys[4], (EXPERTS, D, H), H ** -0.5, 0.3125, ((0, 8),))
    out_grad = normal_values(keys[5], (TOKENS, D), 0.25, 1.5, ((0, 32),))
    return dict(tokens=tokens, expert_ids=expert_ids, gate_scale=gate_scale, w_gate_up=w_gate_up, w_down=w_down, out_grad=out_grad)


def contract_rows(left, right):
    return lax.dot_general(left, right, (((0,), (0,)), ((), ())), preferred_element_type=jnp.float32)


def contract_last(left, right):
    return lax.dot_general(left, right, (((1,), (1,)), ((), ())), preferred_element_type=jnp.float32)


def expert_forward(slot_rows, weight_in, weight_out):
    hidden_units = weight_out.shape[1]
    gate_up = jnp.dot(slot_rows, weight_in, preferred_element_type=jnp.float32)
    gate_part = gate_up[:, :hidden_units]
    up_part = gate_up[:, hidden_units:]
    hidden = (gate_part * jax.nn.sigmoid(gate_part) * up_part).astype(jnp.bfloat16)
    result = contract_last(hidden, weight_out).astype(jnp.bfloat16)
    return gate_part, up_part, hidden, result


def expert_backward(slot_grads, gate_part, up_part, weight_in, weight_out):
    hidden_grad = jnp.dot(slot_grads, weight_out, preferred_element_type=jnp.float32)
    sig_gate = jax.nn.sigmoid(gate_part)
    gate_grad = hidden_grad * up_part * sig_gate * (1.0 + gate_part * (1.0 - sig_gate))
    up_grad = hidden_grad * gate_part * sig_gate
    both_grads = jnp.concatenate([gate_grad, up_grad], axis=1).astype(jnp.bfloat16)
    input_grad = contract_last(both_grads, weight_in).astype(jnp.bfloat16)
    return both_grads, input_grad


def weight_terms(slot_rows, slot_grads, hidden, both_grads):
    return jnp.concatenate([contract_rows(slot_rows, both_grads), contract_rows(slot_grads, hidden)], axis=1)


def reference(tokens, expert_ids, gate_scale, w_gate_up, w_down, out_grad):
    group_rows = N_EXPERT * ROWS_DEV
    all_tokens = tokens.reshape(N_DP, group_rows, D)
    all_ids = expert_ids[:, 0].reshape(N_DP, group_rows)
    all_gates = gate_scale.reshape(N_DP, group_rows)
    all_grads = out_grad.reshape(N_DP, group_rows, D)
    expert_range = jnp.arange(EXPERTS, dtype=jnp.int32)
    block_range = jnp.arange(BLOCK, dtype=jnp.int32)

    def group_step(total, group):
        g_tokens, g_ids, g_gates, g_grads = group
        scaled = (g_gates[:, None] * g_grads.astype(jnp.float32)).astype(jnp.bfloat16)
        order = jnp.argsort(g_ids, stable=True).astype(jnp.int32)
        counts = jnp.sum((g_ids[:, None] == expert_range[None, :]).astype(jnp.int32), axis=0).astype(jnp.int32)
        starts = (jnp.cumsum(counts) - counts).astype(jnp.int32)
        padding = jnp.zeros((BLOCK, D), jnp.bfloat16)
        sorted_rows = jnp.concatenate([g_tokens[order], padding], axis=0)
        sorted_grads = jnp.concatenate([scaled[order], padding], axis=0)
        empty = jnp.zeros((group_rows + BLOCK, D), jnp.bfloat16)

        def expert_step(expert, carry):
            result_buffer, ingrad_buffer, running = carry
            weight_in = lax.dynamic_index_in_dim(w_gate_up, expert, 0, keepdims=False)
            weight_out = lax.dynamic_index_in_dim(w_down, expert, 0, keepdims=False)
            row_total = counts[expert]
            first_row = starts[expert]

            def block_step(block_index, inner):
                result_buffer, ingrad_buffer, partial_value = inner
                row_start = (first_row + block_index * BLOCK).astype(jnp.int32)
                keep_rows = ((block_index * BLOCK + block_range) < row_total)[:, None]
                block_rows = jnp.where(keep_rows, lax.dynamic_slice_in_dim(sorted_rows, row_start, BLOCK, 0), jnp.zeros((), jnp.bfloat16))
                block_grads = jnp.where(keep_rows, lax.dynamic_slice_in_dim(sorted_grads, row_start, BLOCK, 0), jnp.zeros((), jnp.bfloat16))
                gate_part, up_part, hidden, result = expert_forward(block_rows, weight_in, weight_out)
                both_grads, input_grad = expert_backward(block_grads, gate_part, up_part, weight_in, weight_out)
                old_result = lax.dynamic_slice_in_dim(result_buffer, row_start, BLOCK, 0)
                old_ingrad = lax.dynamic_slice_in_dim(ingrad_buffer, row_start, BLOCK, 0)
                result_buffer = lax.dynamic_update_slice_in_dim(result_buffer, jnp.where(keep_rows, result, old_result), row_start, 0)
                ingrad_buffer = lax.dynamic_update_slice_in_dim(ingrad_buffer, jnp.where(keep_rows, input_grad, old_ingrad), row_start, 0)
                partial_value = partial_value + weight_terms(block_rows, block_grads, hidden, both_grads)
                return result_buffer, ingrad_buffer, partial_value

            block_count = ((row_total + BLOCK - 1) // BLOCK).astype(jnp.int32)
            result_buffer, ingrad_buffer, partial_value = lax.fori_loop(
                0, block_count, block_step,
                (result_buffer, ingrad_buffer, jnp.zeros((D, 3 * H), jnp.float32)))
            rounded = lax.optimization_barrier(partial_value.astype(jnp.bfloat16)).astype(jnp.float32)
            current = lax.dynamic_index_in_dim(running, expert, 0, keepdims=False)
            running = lax.dynamic_update_index_in_dim(running, current + rounded, expert, 0)
            return result_buffer, ingrad_buffer, running

        result_buffer, ingrad_buffer, total = lax.fori_loop(0, EXPERTS, expert_step, (empty, empty, total))
        ffn = jnp.zeros((group_rows, D), jnp.bfloat16).at[order].set(result_buffer[:group_rows])
        input_rows = jnp.zeros((group_rows, D), jnp.bfloat16).at[order].set(ingrad_buffer[:group_rows])
        ffn_wide = ffn.astype(jnp.float32)
        mixed = (g_gates[:, None] * ffn_wide).astype(jnp.bfloat16)
        gate_grad_rows = jnp.sum(g_grads.astype(jnp.float32) * ffn_wide, axis=1)
        return total, (mixed, input_rows, gate_grad_rows)

    start_total = jnp.zeros((EXPERTS, D, 3 * H), jnp.float32)
    total, outputs = lax.scan(group_step, start_total, (all_tokens, all_ids, all_gates, all_grads))
    mixed, input_rows, gate_grad_rows = outputs
    return (mixed.reshape(TOKENS, D), input_rows.reshape(TOKENS, D), gate_grad_rows.reshape(TOKENS),
            total[:, :, :2 * H], total[:, :, 2 * H:])
```

```python
import functools

import jax
import jax.numpy as jnp
from jax import lax
from jax.experimental import pallas as pl
from jax.experimental.pallas import tpu as pltpu
from jax.sharding import PartitionSpec as P

F32 = jnp.float32
BF16 = jnp.bfloat16
MESH = pl.DeviceIdType.MESH


def dot(left, right):
    return jnp.dot(left, right, preferred_element_type=F32)


def dot_last(left, right):
    return lax.dot_general(left, right, (((1,), (1,)), ((), ())), preferred_element_type=F32)


def dot_rows(left, right):
    return lax.dot_general(left, right, (((0,), (0,)), ((), ())), preferred_element_type=F32)


def flat_rows(value):
    lead, cap, width = value.shape
    if cap % 16:
        return value.astype(F32).reshape(lead * cap, width).astype(BF16)
    return value.reshape(lead * cap, width)


def kernel(
    n, n_dp, cap,
    tokens, ids, gate_row, w_in_hbm, w_out_hbm, out_grad,
    mixed, input_rows, gate_grad, grad_in, grad_out,
    w_in, w_out, sbuf, rbuf, obuf, gbuf, both_buf, hid_buf,
    wacc, wsend1, wrecv1, wsend2, wrecv2,
    w_sem, s_sem, r_sem, os_sem, or_sem, ws1, wr1, ws2, wr2,
):
    rows, width = tokens.shape
    hidden_units = w_out.shape[1]
    slots = n * cap
    me = lax.axis_index("expert")
    dp = lax.axis_index("dp")
    half = n_dp // 2
    core = lax.rem(dp, 2)
    pair = lax.div(dp, 2)
    other = dp + 1 - 2 * core

    copy_in = pltpu.make_async_copy(w_in_hbm.at[0], w_in, w_sem.at[0])
    copy_out = pltpu.make_async_copy(w_out_hbm.at[0], w_out, w_sem.at[1])
    copy_in.start()
    copy_out.start()

    barrier = pltpu.get_barrier_semaphore()
    for k in range(1, n):
        pl.semaphore_signal(barrier, inc=1, device_id={"expert": lax.rem(me + k, n)}, device_id_type=MESH)
    pl.semaphore_signal(barrier, inc=1, device_id={"dp": other}, device_id_type=MESH)
    for j in range(1, half):
        pl.semaphore_signal(barrier, inc=1, device_id={"dp": lax.rem(dp + 2 * j, n_dp)}, device_id_type=MESH)

    lane = lax.broadcasted_iota(jnp.int32, (rows, rows), 1)
    line = lax.broadcasted_iota(jnp.int32, (rows, rows), 0)
    eye = lane == line
    onehot = jnp.where(lane == ids[...], 1.0, 0.0)
    lower = jnp.where(lane < line, 1.0, 0.0).astype(BF16)
    before = dot(lower, onehot.astype(BF16))
    position = jnp.sum(before * onehot, axis=1, keepdims=True)
    slot_col = ids[...].astype(F32) * float(cap) + position
    slot_row = jnp.sum(jnp.where(eye, slot_col, 0.0), axis=0, keepdims=True)
    gate = jnp.sum(jnp.where(eye, gate_row[...], 0.0), axis=1, keepdims=True)
    slot_line = lax.broadcasted_iota(jnp.int32, (slots, rows), 0)
    places = jnp.where(slot_line == slot_row.astype(jnp.int32), 1.0, 0.0).astype(BF16)
    scaled = (gate * out_grad[...].astype(F32)).astype(BF16)
    sbuf[:, :, :width] = dot(places, tokens[...]).reshape(n, cap, width).astype(BF16)
    sbuf[:, :, width:] = dot(places, scaled).reshape(n, cap, width).astype(BF16)
    rbuf[pl.ds(me, 1)] = sbuf[pl.ds(me, 1)]

    pl.semaphore_wait(barrier, n - 1 + half)

    def dispatch(peer):
        return pltpu.make_async_remote_copy(
            src_ref=sbuf.at[peer], dst_ref=rbuf.at[me],
            send_sem=s_sem.at[peer], recv_sem=r_sem.at[me],
            device_id={"expert": peer}, device_id_type=MESH)

    def arrival(peer):
        return pltpu.make_async_remote_copy(
            src_ref=sbuf.at[peer], dst_ref=rbuf.at[peer],
            send_sem=s_sem.at[peer], recv_sem=r_sem.at[peer],
            device_id={"expert": peer}, device_id_type=MESH)

    def give_back(peer):
        return pltpu.make_async_remote_copy(
            src_ref=obuf.at[peer], dst_ref=gbuf.at[me],
            send_sem=os_sem.at[peer], recv_sem=or_sem.at[me],
            device_id={"expert": peer}, device_id_type=MESH)

    def got_back(peer):
        return pltpu.make_async_remote_copy(
            src_ref=obuf.at[peer], dst_ref=gbuf.at[peer],
            send_sem=os_sem.at[peer], recv_sem=or_sem.at[peer],
            device_id={"expert": peer}, device_id_type=MESH)

    def offset(k):
        return lax.rem(jnp.where(lax.rem(k, 2) == 1, (k + 1) // 2, n - k // 2), n)

    for k in range(n - 1, 0, -1):
        off = (k + 1) // 2 if k % 2 else n - k // 2
        dispatch(lax.rem(me + off, n)).start()

    copy_in.wait()
    copy_out.wait()

    def chunk(source, keep):
        block = rbuf[source]
        gate_up = dot(block[:, :width], w_in[...])
        gate_part = gate_up[:, :hidden_units]
        up_part = gate_up[:, hidden_units:]
        sig = jax.nn.sigmoid(gate_part)
        hidden = (gate_part * sig * up_part).astype(BF16)
        hidden_grad = dot(block[:, width:], w_out[...])
        gate_grad_part = hidden_grad * up_part * sig * (1.0 + gate_part * (1.0 - sig))
        up_grad = hidden_grad * gate_part * sig
        both = jnp.concatenate([gate_grad_part, up_grad], axis=1).astype(BF16)
        hid_buf[source] = hidden
        both_buf[source] = both
        keep[source, :, :width] = dot_last(hidden, w_out[...]).astype(BF16)
        keep[source, :, width:] = dot_last(both, w_in[...]).astype(BF16)

    chunk(me, gbuf)

    def one_source(k, carry):
        source = lax.rem(me + offset(k), n)
        arrival(source).wait_recv()
        chunk(source, obuf)
        give_back(source).start()
        return carry

    lax.fori_loop(1, n, one_source, 0)

    both_all = flat_rows(both_buf[...])
    hid_all = flat_rows(hid_buf[...])
    x_all = flat_rows(rbuf[:, :, :width])
    g_all = flat_rows(rbuf[:, :, width:])
    part = width // n_dp
    wacc[:, :, : 2 * hidden_units] = dot_rows(x_all, both_all).reshape(n_dp, part, 2 * hidden_units)
    wacc[:, :, 2 * hidden_units :] = dot_rows(g_all, hid_all).reshape(n_dp, part, hidden_units)

    def pair_copy(j):
        return pltpu.make_async_remote_copy(
            src_ref=wsend1.at[j], dst_ref=wrecv1.at[j],
            send_sem=ws1.at[j], recv_sem=wr1.at[j],
            device_id={"dp": other}, device_id_type=MESH)

    for k in range(half):
        j = lax.rem(pair + 1 + k, half)
        wsend1[j] = wacc[2 * j + 1 - core].astype(BF16)
        pair_copy(j).start()

    def far_copy(j):
        return pltpu.make_async_remote_copy(
            src_ref=wsend2.at[j], dst_ref=wrecv2.at[pair],
            send_sem=ws2.at[j], recv_sem=wr2.at[pair],
            device_id={"dp": 2 * j + core}, device_id_type=MESH)

    def far_arrival(j):
        return pltpu.make_async_remote_copy(
            src_ref=wsend2.at[j], dst_ref=wrecv2.at[j],
            send_sem=ws2.at[j], recv_sem=wr2.at[j],
            device_id={"dp": 2 * j + core}, device_id_type=MESH)

    for k in range(1, half):
        j = lax.rem(pair + k, half)
        pair_copy(j).wait_recv()
        wsend2[j] = (wacc[2 * j + core] + wrecv1[j].astype(F32)).astype(BF16)
        far_copy(j).start()
    pair_copy(pair).wait_recv()
    total = wacc[dp] + wrecv1[pair].astype(F32)
    for k in range(1, half):
        j = lax.rem(pair + k, half)
        far_arrival(j).wait_recv()
        total = total + wrecv2[j].astype(F32)
    grad_in[0] = total[:, : 2 * hidden_units]
    grad_out[0] = total[:, 2 * hidden_units :]

    for k in range(1, n):
        got_back(lax.rem(me + k, n)).wait_recv()
    slot_lane = lax.broadcasted_iota(jnp.int32, (rows, slots), 1)
    picks = jnp.where(slot_lane == slot_col.astype(jnp.int32), 1.0, 0.0).astype(BF16)
    ffn = dot(picks, flat_rows(gbuf[:, :, :width]))
    mixed[...] = (gate * ffn).astype(BF16)
    sums = jnp.sum(out_grad[...].astype(F32) * ffn, axis=1, keepdims=True)
    gate_grad[...] = jnp.sum(jnp.where(eye, sums, 0.0), axis=0, keepdims=True)
    input_rows[...] = dot(picks, flat_rows(gbuf[:, :, width:])).astype(BF16)

    for k in range(1, n):
        peer = lax.rem(me + k, n)
        dispatch(peer).wait_send()
        give_back(peer).wait_send()
    for j in range(half):
        pair_copy(j).wait_send()
    for k in range(1, half):
        far_copy(lax.rem(pair + k, half)).wait_send()


def on_device(n, n_dp, tokens, expert_ids, gate_scale, w_gate_up, w_down, out_grad):
    rows, width = tokens.shape
    hidden_units = w_down.shape[2]
    cap = 3 * rows // n
    part = width // n_dp
    half = n_dp // 2
    terms = 3 * hidden_units
    vmem = pl.BlockSpec(memory_space=pltpu.VMEM)
    anywhere = pl.BlockSpec(memory_space=pl.ANY)
    dma = pltpu.SemaphoreType.DMA
    mixed, input_rows, gate_grad, grad_in, grad_out = pl.pallas_call(
        functools.partial(kernel, n, n_dp, cap),
        out_shape=(
            jax.ShapeDtypeStruct((rows, width), BF16),
            jax.ShapeDtypeStruct((rows, width), BF16),
            jax.ShapeDtypeStruct((1, rows), F32),
            jax.ShapeDtypeStruct((1, part, 2 * hidden_units), F32),
            jax.ShapeDtypeStruct((1, part, hidden_units), F32),
        ),
        in_specs=[vmem, vmem, vmem, anywhere, anywhere, vmem],
        out_specs=(vmem,) * 5,
        scratch_shapes=[
            pltpu.VMEM((width, 2 * hidden_units), BF16),
            pltpu.VMEM((width, hidden_units), BF16),
            pltpu.VMEM((n, cap, 2 * width), BF16),
            pltpu.VMEM((n, cap, 2 * width), BF16),
            pltpu.VMEM((n, cap, 2 * width), BF16),
            pltpu.VMEM((n, cap, 2 * width), BF16),
            pltpu.VMEM((n, cap, 2 * hidden_units), BF16),
            pltpu.VMEM((n, cap, hidden_units), BF16),
            pltpu.VMEM((n_dp, part, terms), F32),
            pltpu.VMEM((half, part, terms), BF16),
            pltpu.VMEM((half, part, terms), BF16),
            pltpu.VMEM((half, part, terms), BF16),
            pltpu.VMEM((half, part, terms), BF16),
            dma((2,)), dma((n,)), dma((n,)), dma((n,)), dma((n,)),
            dma((half,)), dma((half,)), dma((half,)), dma((half,)),
        ],
        compiler_params=pltpu.CompilerParams(
            collective_id=0, has_side_effects=True, vmem_limit_bytes=56 * 1024 * 1024),
    )(tokens, expert_ids, gate_scale[None, :], w_gate_up, w_down, out_grad)
    return mixed, input_rows, gate_grad[0], grad_in, grad_out


def solution(mesh):
    return jax.shard_map(
        functools.partial(on_device, mesh.shape["expert"], mesh.shape["dp"]),
        mesh=mesh,
        in_specs=(
            P(("dp", "expert"), None),
            P(("dp", "expert"), None),
            P(("dp", "expert")),
            P("expert", None, None),
            P("expert", None, None),
            P(("dp", "expert"), None),
        ),
        out_specs=(
            P(("dp", "expert"), None),
            P(("dp", "expert"), None),
            P(("dp", "expert")),
            P("expert", "dp", None),
            P("expert", "dp", None),
        ),
        check_vma=False,
    )
```

```python
import functools

import jax
import jax.numpy as jnp
from jax import lax
from jax.experimental import pallas as pl
from jax.experimental.pallas import tpu as pltpu
from jax.sharding import PartitionSpec as P

F32 = jnp.float32
BF16 = jnp.bfloat16
MESH = pl.DeviceIdType.MESH


def dot(left, right):
    return jnp.dot(left, right, preferred_element_type=F32)


def dot_last(left, right):
    return lax.dot_general(left, right, (((1,), (1,)), ((), ())), preferred_element_type=F32)


def dot_rows(left, right):
    return lax.dot_general(left, right, (((0,), (0,)), ((), ())), preferred_element_type=F32)


def flat_rows(value):
    lead, cap, width = value.shape
    if cap % 16:
        return value.astype(F32).reshape(lead * cap, width).astype(BF16)
    return value.reshape(lead * cap, width)


def kernel(
    n, n_dp, cap, cuts,
    tokens, ids_row, gate_row, w_in_hbm, w_out_hbm, out_grad,
    mixed, input_rows, gate_grad, grad_in, grad_out,
    w_in, w_out, scaled_buf, info, info_got, raw_got, own_send, far_send, rbuf, obuf,
    own_back, far_back, relay_send, relay_back, gate_up_buf, both_buf, hid_buf,
    wacc, wsend1, wrecv1, wsend2, wrecv2,
    w_sem, is_sem, ir_sem, raw_s, raw_r, own_s, own_r, far_s, far_r,
    ob_s, ob_r, fb_s, fb_r, rb_s, rb_r, ws1, wr1, ws2, wr2,
):
    rows, width = tokens.shape
    hidden_units = w_out.shape[1]
    piece = width // cuts
    h = n // 2
    relays = h // 2
    me = lax.axis_index("expert")
    dp = lax.axis_index("dp")
    half = n_dp // 2
    core = lax.rem(dp, 2)
    pair = lax.div(dp, 2)
    other = dp + 1 - 2 * core
    upper = lax.div(me, h)
    base = upper * h
    mine = me - base
    my_relay = lax.rem(mine, relays)
    my_lane = lax.div(mine, relays)
    relay_start = base + (1 - upper) * relays
    far_relay = (1 - upper) * h + upper * relays + my_relay
    is_relay = lax.div(mine, relays) == 1 - upper
    far_base = (1 - upper) * h

    def remote(source, target, send, receive, peer):
        return pltpu.make_async_remote_copy(
            src_ref=source, dst_ref=target, send_sem=send, recv_sem=receive,
            device_id={"expert": peer}, device_id_type=MESH)

    copy_in = pltpu.make_async_copy(w_in_hbm.at[0], w_in, w_sem.at[0])
    copy_out = pltpu.make_async_copy(w_out_hbm.at[0], w_out, w_sem.at[1])
    copy_in.start()
    copy_out.start()

    barrier = pltpu.get_barrier_semaphore()
    for k in range(1, n):
        pl.semaphore_signal(barrier, inc=1, device_id={"expert": lax.rem(me + k, n)}, device_id_type=MESH)
    pl.semaphore_signal(barrier, inc=1, device_id={"dp": other}, device_id_type=MESH)
    for j in range(1, half):
        pl.semaphore_signal(barrier, inc=1, device_id={"dp": lax.rem(dp + 2 * j, n_dp)}, device_id_type=MESH)

    lane = lax.broadcasted_iota(jnp.int32, (rows, rows), 1)
    line = lax.broadcasted_iota(jnp.int32, (rows, rows), 0)
    eye = lane == line
    ids_f = ids_row[...].astype(F32)
    ids_col = jnp.sum(jnp.where(eye, ids_f, 0.0), axis=1, keepdims=True)
    onehot = jnp.where(lane.astype(F32) == ids_col, 1.0, 0.0)
    lower = jnp.where(lane < line, 1.0, 0.0).astype(BF16)
    before = dot(lower, onehot.astype(BF16))
    position = jnp.sum(before * onehot, axis=1, keepdims=True)
    slot_col = ids_col * float(cap) + position
    slot_row = jnp.sum(jnp.where(eye, slot_col, 0.0), axis=0, keepdims=True)
    info[...] = jnp.broadcast_to(slot_row, info.shape)
    gate = jnp.sum(jnp.where(eye, gate_row[...], 0.0), axis=1, keepdims=True)
    scaled_buf[...] = (gate * out_grad[...].astype(F32)).astype(BF16)

    def place_rows(row):
        spot = lax.broadcasted_iota(jnp.int32, (h * cap, rows), 0) + base * cap
        return jnp.where(spot == row.astype(jnp.int32), 1.0, 0.0).astype(BF16)

    def pick_rows(col):
        spot = lax.broadcasted_iota(jnp.int32, (rows, h * cap), 1) + base * cap
        return jnp.where(spot == col.astype(jnp.int32), 1.0, 0.0).astype(BF16)

    def columns(ref, p):
        q = p % cuts
        return ref.at[:, pl.ds(q * piece, piece)]

    def raw_source(p):
        return columns(tokens if p < cuts else scaled_buf, p)

    def raw_copy(p):
        return remote(raw_source(p), raw_got.at[p, my_lane], raw_s.at[p], raw_r.at[p, my_lane], far_relay)

    def raw_arrival(p, f):
        return remote(raw_source(p), raw_got.at[p, f], raw_s.at[p], raw_r.at[p, f], far_relay)

    def own_copy(p, i):
        return remote(own_send.at[p, i], rbuf.at[p, mine], own_s.at[p, i], own_r.at[p, mine], base + i)

    def own_arrival(p, i):
        return remote(own_send.at[p, i], rbuf.at[p, i], own_s.at[p, i], own_r.at[p, i], base + i)

    def far_copy(p, i):
        return remote(far_send.at[p, i], rbuf.at[p, pl.ds(h + 2 * my_relay, 2)],
                      far_s.at[p, i], far_r.at[p, my_relay], base + i)

    def far_arrival(p, r):
        return remote(far_send.at[p, 0], rbuf.at[p, pl.ds(h + 2 * r, 2)],
                      far_s.at[p, 0], far_r.at[p, r], relay_start + r)

    def own_return(p, i):
        return remote(obuf.at[p, i], own_back.at[p, mine], ob_s.at[p, i], ob_r.at[p, mine], base + i)

    def own_returned(p, i):
        return remote(obuf.at[p, i], own_back.at[p, i], ob_s.at[p, i], ob_r.at[p, i], base + i)

    def far_return(p, r):
        return remote(obuf.at[p, pl.ds(h + 2 * r, 2)], far_back.at[p, mine],
                      fb_s.at[p, r], fb_r.at[p, mine], relay_start + r)

    def far_returned(p, i):
        return remote(obuf.at[p, pl.ds(h, 2)], far_back.at[p, i], fb_s.at[p, 0], fb_r.at[p, i], base + i)

    def relay_copy(p, f):
        return remote(relay_send.at[p, f], relay_back.at[p], rb_s.at[p, f], rb_r.at[p],
                      far_base + f * relays + my_relay)

    def relayed(p):
        return remote(relay_send.at[p, 0], relay_back.at[p], rb_s.at[p, 0], rb_r.at[p], far_relay)

    def info_copy():
        return remote(info, info_got.at[my_lane], is_sem.at[0], ir_sem.at[my_lane], far_relay)

    def info_arrival(f):
        return remote(info, info_got.at[f], is_sem.at[0], ir_sem.at[f], far_relay)

    front, rear = range(cuts), range(cuts, 2 * cuts)
    every = range(2 * cuts)
    own_places = place_rows(slot_row)
    pl.semaphore_wait(barrier, n - 1 + half)
    info_copy().start()
    for part in (front, rear):
        for p in part:
            raw_copy(p).start()
        for p in part:
            own_send[p] = dot(own_places, raw_source(p)[...]).reshape(h, cap, piece).astype(BF16)
            for k in range(1, h):
                own_copy(p, lax.rem(mine + k, h)).start()
            rbuf[p, pl.ds(mine, 1)] = own_send[p, pl.ds(mine, 1)]

    copy_in.wait()
    copy_out.wait()

    def forward(slot, count):
        span = pl.ds(slot, count)
        gate_up = dot(flat_rows(rbuf[0, span]), w_in[:piece])
        for p in front[1:]:
            gate_up += dot(flat_rows(rbuf[p, span]), w_in[p * piece : (p + 1) * piece])
        gate_part = gate_up[:, :hidden_units]
        up_part = gate_up[:, hidden_units:]
        hidden = gate_part * jax.nn.sigmoid(gate_part) * up_part
        gate_up_buf[span] = gate_up.reshape(count, cap, 2 * hidden_units)
        hid_buf[span] = hidden.reshape(count, cap, hidden_units).astype(BF16)
        hidden = hidden.astype(BF16)
        for p in front:
            value = dot_last(hidden, w_out[p * piece : (p + 1) * piece])
            obuf[p, span] = value.reshape(count, cap, piece).astype(BF16)

    def backward(slot, count):
        span = pl.ds(slot, count)
        hidden_grad = dot(flat_rows(rbuf[cuts, span]), w_out[:piece])
        for q in front[1:]:
            hidden_grad += dot(flat_rows(rbuf[cuts + q, span]), w_out[q * piece : (q + 1) * piece])
        gate_up = gate_up_buf[span].reshape(count * cap, 2 * hidden_units)
        gate_part = gate_up[:, :hidden_units]
        up_part = gate_up[:, hidden_units:]
        sig = jax.nn.sigmoid(gate_part)
        gate_term = hidden_grad * up_part * sig * (1.0 + gate_part * (1.0 - sig))
        up_term = hidden_grad * gate_part * sig
        both = jnp.concatenate([gate_term, up_term], axis=1)
        both_buf[span] = both.reshape(count, cap, 2 * hidden_units).astype(BF16)
        both = both.astype(BF16)
        for q in front:
            value = dot_last(both, w_in[q * piece : (q + 1) * piece])
            obuf[cuts + q, span] = value.reshape(count, cap, piece).astype(BF16)

    def own_pass(work, part):
        work(mine, 1)
        for p in part:
            own_back[p, pl.ds(mine, 1)] = obuf[p, pl.ds(mine, 1)]

        def one(k, carry):
            i = lax.rem(mine + k, h)
            for p in part:
                own_arrival(p, i).wait_recv()
            work(i, 1)
            for p in part:
                own_return(p, i).start()
            return carry

        lax.fori_loop(1, h, one, 0)

    def far_pass(work, part):
        def one(k, carry):
            r = lax.rem(my_relay + k, relays)
            myself = jnp.logical_and(is_relay, r == my_relay)

            @pl.when(jnp.logical_not(myself))
            def _():
                for p in part:
                    far_arrival(p, r).wait_recv()

            work(h + 2 * r, 2)

            @pl.when(myself)
            def _():
                for p in part:
                    far_back[p, mine] = obuf[p, pl.ds(h + 2 * r, 2)]

            @pl.when(jnp.logical_not(myself))
            def _():
                for p in part:
                    far_return(p, r).start()

            return carry

        lax.fori_loop(0, relays, one, 0)

    def relay_out(p):
        @pl.when(is_relay)
        def _():
            for f in range(2):
                if p == 0:
                    info_arrival(f).wait_recv()
                raw_arrival(p, f).wait_recv()
                value = dot(place_rows(info_got[f, :1, :]), raw_got[p, f])
                far_send[p, :, f] = value.reshape(h, cap, piece).astype(BF16)
            for k in range(1, h):
                far_copy(p, lax.rem(mine + k, h)).start()
            rbuf[p, pl.ds(h + 2 * my_relay, 2)] = far_send[p, mine]

    def relay_in(part):
        @pl.when(is_relay)
        def _():
            picks = []
            for f in range(2):
                col = jnp.sum(jnp.where(eye, info_got[f, :1, :], 0.0), axis=1, keepdims=True)
                picks.append(pick_rows(col))
            for p in part:
                for k in range(1, h):
                    far_returned(p, lax.rem(mine + k, h)).wait_recv()
                for f in range(2):
                    relay_send[p, f] = dot(picks[f], flat_rows(far_back[p, :, f])).astype(BF16)
                    relay_copy(p, f).start()

    own_pass(forward, front)
    for p in front:
        relay_out(p)
    own_pass(backward, rear)
    for p in rear[:-1]:
        relay_out(p)
    far_pass(forward, front)
    relay_out(rear[-1])
    relay_in(front)
    far_pass(backward, rear)

    both_all = flat_rows(both_buf[...])
    hid_all = flat_rows(hid_buf[...])
    share = width // n_dp
    blocks = n_dp // cuts
    for q in front:
        into = pl.ds(q * blocks, blocks)
        wacc[into, :, : 2 * hidden_units] = dot_rows(flat_rows(rbuf[q]), both_all).reshape(
            blocks, share, 2 * hidden_units)
        wacc[into, :, 2 * hidden_units :] = dot_rows(flat_rows(rbuf[cuts + q]), hid_all).reshape(
            blocks, share, hidden_units)

    def pair_copy(j):
        return pltpu.make_async_remote_copy(
            src_ref=wsend1.at[j], dst_ref=wrecv1.at[j],
            send_sem=ws1.at[j], recv_sem=wr1.at[j],
            device_id={"dp": other}, device_id_type=MESH)

    for k in range(half):
        j = lax.rem(pair + 1 + k, half)
        wsend1[j] = wacc[2 * j + 1 - core].astype(BF16)
        pair_copy(j).start()

    def group_copy(j):
        return pltpu.make_async_remote_copy(
            src_ref=wsend2.at[j], dst_ref=wrecv2.at[pair],
            send_sem=ws2.at[j], recv_sem=wr2.at[pair],
            device_id={"dp": 2 * j + core}, device_id_type=MESH)

    def group_arrival(j):
        return pltpu.make_async_remote_copy(
            src_ref=wsend2.at[j], dst_ref=wrecv2.at[j],
            send_sem=ws2.at[j], recv_sem=wr2.at[j],
            device_id={"dp": 2 * j + core}, device_id_type=MESH)

    for k in range(1, half):
        j = lax.rem(pair + k, half)
        pair_copy(j).wait_recv()
        wsend2[j] = (wacc[2 * j + core] + wrecv1[j].astype(F32)).astype(BF16)
        group_copy(j).start()

    relay_in(rear)

    picks = pick_rows(slot_col)
    for k in range(1, h):
        for p in every:
            own_returned(p, lax.rem(mine + k, h)).wait_recv()
    sums = jnp.zeros((rows, 1), F32)
    for p in front:
        into = pl.ds(p * piece, piece)
        relayed(p).wait_recv()
        ffn = dot(picks, flat_rows(own_back[p])) + relay_back[p].astype(F32)
        mixed[:, into] = (gate * ffn).astype(BF16)
        sums += jnp.sum(out_grad[:, into].astype(F32) * ffn, axis=1, keepdims=True)
    gate_grad[...] = jnp.sum(jnp.where(eye, sums, 0.0), axis=0, keepdims=True)

    pair_copy(pair).wait_recv()
    total = wacc[dp] + wrecv1[pair].astype(F32)
    for k in range(1, half):
        j = lax.rem(pair + k, half)
        group_arrival(j).wait_recv()
        total = total + wrecv2[j].astype(F32)
    grad_in[0] = total[:, : 2 * hidden_units]
    grad_out[0] = total[:, 2 * hidden_units :]

    for q in front:
        p = cuts + q
        relayed(p).wait_recv()
        value = dot(picks, flat_rows(own_back[p])) + relay_back[p].astype(F32)
        input_rows[:, pl.ds(q * piece, piece)] = value.astype(BF16)

    info_copy().wait_send()
    for p in every:
        raw_copy(p).wait_send()
        for k in range(1, h):
            i = lax.rem(mine + k, h)
            own_copy(p, i).wait_send()
            own_return(p, i).wait_send()
        for r in range(relays):
            @pl.when(jnp.logical_not(jnp.logical_and(is_relay, my_relay == r)))
            def _():
                far_return(p, r).wait_send()

    @pl.when(is_relay)
    def _():
        for p in every:
            for k in range(1, h):
                far_copy(p, lax.rem(mine + k, h)).wait_send()
            for f in range(2):
                relay_copy(p, f).wait_send()
    for j in range(half):
        pair_copy(j).wait_send()
    for k in range(1, half):
        group_copy(lax.rem(pair + k, half)).wait_send()


def pass_on(*refs):
    count = len(refs) // 2
    for source, target in zip(refs[:count], refs[count:]):
        target[...] = source[...]


def on_device(n, n_dp, tokens, expert_ids, gate_scale, w_gate_up, w_down, out_grad):
    rows, width = tokens.shape
    hidden_units = w_down.shape[2]
    cap = 3 * rows // n
    share = width // n_dp
    half = n_dp // 2
    terms = 3 * hidden_units
    cuts = 2
    piece = width // cuts
    both = 2 * cuts
    h = n // 2
    relays = h // 2
    vmem = pl.BlockSpec(memory_space=pltpu.VMEM)
    anywhere = pl.BlockSpec(memory_space=pl.ANY)
    dma = pltpu.SemaphoreType.DMA
    shapes = (
        jax.ShapeDtypeStruct((rows, width), BF16),
        jax.ShapeDtypeStruct((rows, width), BF16),
        jax.ShapeDtypeStruct((1, rows), F32),
        jax.ShapeDtypeStruct((1, share, 2 * hidden_units), F32),
        jax.ShapeDtypeStruct((1, share, hidden_units), F32),
    )
    results = pl.pallas_call(
        functools.partial(kernel, n, n_dp, cap, cuts),
        out_shape=shapes,
        in_specs=[vmem, vmem, vmem, anywhere, anywhere, vmem],
        out_specs=(vmem,) * 5,
        scratch_shapes=[
            pltpu.VMEM((width, 2 * hidden_units), BF16),
            pltpu.VMEM((width, hidden_units), BF16),
            pltpu.VMEM((rows, width), BF16),
            pltpu.VMEM((8, rows), F32),
            pltpu.VMEM((2, 8, rows), F32),
            pltpu.VMEM((both, 2, rows, piece), BF16),
            pltpu.VMEM((both, h, cap, piece), BF16),
            pltpu.VMEM((both, h, 2, cap, piece), BF16),
            pltpu.VMEM((both, n, cap, piece), BF16),
            pltpu.VMEM((both, n, cap, piece), BF16),
            pltpu.VMEM((both, h, cap, piece), BF16),
            pltpu.VMEM((both, h, 2, cap, piece), BF16),
            pltpu.VMEM((both, 2, rows, piece), BF16),
            pltpu.VMEM((both, rows, piece), BF16),
            pltpu.VMEM((n, cap, 2 * hidden_units), F32),
            pltpu.VMEM((n, cap, 2 * hidden_units), BF16),
            pltpu.VMEM((n, cap, hidden_units), BF16),
            pltpu.VMEM((n_dp, share, terms), F32),
            pltpu.VMEM((half, share, terms), BF16),
            pltpu.VMEM((half, share, terms), BF16),
            pltpu.VMEM((half, share, terms), BF16),
            pltpu.VMEM((half, share, terms), BF16),
            dma((2,)), dma((1,)), dma((2,)),
            dma((both,)), dma((both, 2)),
            dma((both, h)), dma((both, h)),
            dma((both, h)), dma((both, relays)),
            dma((both, h)), dma((both, h)),
            dma((both, relays)), dma((both, h)),
            dma((both, 2)), dma((both,)),
            dma((half,)), dma((half,)), dma((half,)), dma((half,)),
        ],
        compiler_params=pltpu.CompilerParams(
            collective_id=0, has_side_effects=True, vmem_limit_bytes=48 * 1024 * 1024),
    )(tokens, expert_ids.reshape(1, rows), gate_scale[None, :], w_gate_up, w_down, out_grad)
    mixed, input_rows, gate_grad, grad_in, grad_out = pl.pallas_call(
        pass_on,
        out_shape=shapes,
        in_specs=[vmem] * 5,
        out_specs=(vmem,) * 5,
    )(*results)
    return mixed, input_rows, gate_grad[0], grad_in, grad_out


def solution(mesh):
    return jax.shard_map(
        functools.partial(on_device, mesh.shape["expert"], mesh.shape["dp"]),
        mesh=mesh,
        in_specs=(
            P(("dp", "expert"), None),
            P(("dp", "expert"), None),
            P(("dp", "expert")),
            P("expert", None, None),
            P("expert", None, None),
            P(("dp", "expert"), None),
        ),
        out_specs=(
            P(("dp", "expert"), None),
            P(("dp", "expert"), None),
            P(("dp", "expert")),
            P("expert", "dp", None),
            P("expert", "dp", None),
        ),
        check_vma=False,
    )
```

```python
import functools

import jax
import jax.numpy as jnp
from jax import lax
from jax.experimental import pallas as pl
from jax.experimental.pallas import tpu as pltpu
from jax.sharding import PartitionSpec as P

F32 = jnp.float32
BF16 = jnp.bfloat16
MESH = pl.DeviceIdType.MESH


def dot(left, right):
    return jnp.dot(left, right, preferred_element_type=F32)


def dot_last(left, right):
    return lax.dot_general(left, right, (((1,), (1,)), ((), ())), preferred_element_type=F32)


def dot_rows(left, right):
    return lax.dot_general(left, right, (((0,), (0,)), ((), ())), preferred_element_type=F32)


def flat_rows(value):
    lead, cap, width = value.shape
    if cap % 16:
        return value.astype(F32).reshape(lead * cap, width).astype(BF16)
    return value.reshape(lead * cap, width)


def kernel(
    n, n_dp, cap, cuts,
    tokens_hbm, ids_hbm, gate_hbm, w_in_hbm, w_out_hbm, grad_hbm,
    mixed, input_rows, gate_grad, grad_in, grad_out,
    tokens, ids_row, gate_row, out_grad, w_in, w_out, scaled_buf, info, info_got, raw_got, own_send, far_send, rbuf, obuf,
    own_back, far_back, relay_send, relay_back, gate_up_buf, both_buf, hid_buf,
    wacc, wsend1, wrecv1, wsend2, wrecv2,
    w_sem, is_sem, ir_sem, raw_s, raw_r, own_s, own_r, far_s, far_r,
    ob_s, ob_r, fb_s, fb_r, rb_s, rb_r, ws1, wr1, ws2, wr2,
):
    rows, width = tokens.shape
    hidden_units = w_out.shape[1]
    piece = width // cuts
    h = n // 2
    relays = h // 2
    me = lax.axis_index("expert")
    dp = lax.axis_index("dp")
    half = n_dp // 2
    core = lax.rem(dp, 2)
    pair = lax.div(dp, 2)
    other = dp + 1 - 2 * core
    upper = lax.div(me, h)
    base = upper * h
    mine = me - base
    my_relay = lax.rem(mine, relays)
    my_lane = lax.div(mine, relays)
    relay_start = base + (1 - upper) * relays
    far_relay = (1 - upper) * h + upper * relays + my_relay
    is_relay = lax.div(mine, relays) == 1 - upper
    far_base = (1 - upper) * h

    def remote(source, target, send, receive, peer):
        return pltpu.make_async_remote_copy(
            src_ref=source, dst_ref=target, send_sem=send, recv_sem=receive,
            device_id={"expert": peer}, device_id_type=MESH)

    copy_in = pltpu.make_async_copy(w_in_hbm.at[0], w_in, w_sem.at[0])
    copy_out = pltpu.make_async_copy(w_out_hbm.at[0], w_out, w_sem.at[1])
    loads = [
        pltpu.make_async_copy(source, target, w_sem.at[2 + i])
        for i, (source, target) in enumerate((
            (ids_hbm, ids_row), (gate_hbm, gate_row), (tokens_hbm, tokens), (grad_hbm, out_grad)))
    ]
    for load in loads:
        load.start()
    copy_in.start()
    copy_out.start()

    barrier = pltpu.get_barrier_semaphore()
    for k in range(1, n):
        pl.semaphore_signal(barrier, inc=1, device_id={"expert": lax.rem(me + k, n)}, device_id_type=MESH)
    pl.semaphore_signal(barrier, inc=1, device_id={"dp": other}, device_id_type=MESH)
    for j in range(1, half):
        pl.semaphore_signal(barrier, inc=1, device_id={"dp": lax.rem(dp + 2 * j, n_dp)}, device_id_type=MESH)

    for load in loads:
        load.wait()
    lane = lax.broadcasted_iota(jnp.int32, (rows, rows), 1)
    line = lax.broadcasted_iota(jnp.int32, (rows, rows), 0)
    eye = lane == line
    ids_f = ids_row[...].astype(F32)
    ids_col = jnp.sum(jnp.where(eye, ids_f, 0.0), axis=1, keepdims=True)
    onehot = jnp.where(lane.astype(F32) == ids_col, 1.0, 0.0)
    lower = jnp.where(lane < line, 1.0, 0.0).astype(BF16)
    before = dot(lower, onehot.astype(BF16))
    position = jnp.sum(before * onehot, axis=1, keepdims=True)
    slot_col = ids_col * float(cap) + position
    slot_row = jnp.sum(jnp.where(eye, slot_col, 0.0), axis=0, keepdims=True)
    info[...] = jnp.broadcast_to(slot_row, info.shape)
    gate = jnp.sum(jnp.where(eye, gate_row[...], 0.0), axis=1, keepdims=True)
    scaled_buf[...] = (gate * out_grad[...].astype(F32)).astype(BF16)

    def place_rows(row):
        spot = lax.broadcasted_iota(jnp.int32, (h * cap, rows), 0) + base * cap
        return jnp.where(spot == row.astype(jnp.int32), 1.0, 0.0).astype(BF16)

    def pick_rows(col):
        spot = lax.broadcasted_iota(jnp.int32, (rows, h * cap), 1) + base * cap
        return jnp.where(spot == col.astype(jnp.int32), 1.0, 0.0).astype(BF16)

    def columns(ref, p):
        q = p % cuts
        return ref.at[:, pl.ds(q * piece, piece)]

    def raw_source(p):
        return columns(tokens if p < cuts else scaled_buf, p)

    def raw_copy(p):
        return remote(raw_source(p), raw_got.at[p, my_lane], raw_s.at[p], raw_r.at[p, my_lane], far_relay)

    def raw_arrival(p, f):
        return remote(raw_source(p), raw_got.at[p, f], raw_s.at[p], raw_r.at[p, f], far_relay)

    def own_copy(p, i):
        return remote(own_send.at[p, i], rbuf.at[p, mine], own_s.at[p, i], own_r.at[p, mine], base + i)

    def own_arrival(p, i):
        return remote(own_send.at[p, i], rbuf.at[p, i], own_s.at[p, i], own_r.at[p, i], base + i)

    def far_copy(p, i):
        return remote(far_send.at[p, i], rbuf.at[p, pl.ds(h + 2 * my_relay, 2)],
                      far_s.at[p, i], far_r.at[p, my_relay], base + i)

    def far_arrival(p, r):
        return remote(far_send.at[p, 0], rbuf.at[p, pl.ds(h + 2 * r, 2)],
                      far_s.at[p, 0], far_r.at[p, r], relay_start + r)

    def own_return(p, i):
        return remote(obuf.at[p, i], own_back.at[p, mine], ob_s.at[p, i], ob_r.at[p, mine], base + i)

    def own_returned(p, i):
        return remote(obuf.at[p, i], own_back.at[p, i], ob_s.at[p, i], ob_r.at[p, i], base + i)

    def far_return(p, r):
        return remote(obuf.at[p, pl.ds(h + 2 * r, 2)], far_back.at[p, mine],
                      fb_s.at[p, r], fb_r.at[p, mine], relay_start + r)

    def far_returned(p, i):
        return remote(obuf.at[p, pl.ds(h, 2)], far_back.at[p, i], fb_s.at[p, 0], fb_r.at[p, i], base + i)

    def relay_copy(p, f):
        return remote(relay_send.at[p, f], relay_back.at[p], rb_s.at[p, f], rb_r.at[p],
                      far_base + f * relays + my_relay)

    def relayed(p):
        return remote(relay_send.at[p, 0], relay_back.at[p], rb_s.at[p, 0], rb_r.at[p], far_relay)

    def info_copy():
        return remote(info, info_got.at[my_lane], is_sem.at[0], ir_sem.at[my_lane], far_relay)

    def info_arrival(f):
        return remote(info, info_got.at[f], is_sem.at[0], ir_sem.at[f], far_relay)

    front, rear = range(cuts), range(cuts, 2 * cuts)
    every = range(2 * cuts)
    own_places = place_rows(slot_row)
    pl.semaphore_wait(barrier, n - 1 + half)
    info_copy().start()
    for part in (front, rear):
        for p in part:
            raw_copy(p).start()
        for p in part:
            own_send[p] = dot(own_places, raw_source(p)[...]).reshape(h, cap, piece).astype(BF16)
            for k in range(1, h):
                own_copy(p, lax.rem(mine + k, h)).start()
            rbuf[p, pl.ds(mine, 1)] = own_send[p, pl.ds(mine, 1)]

    copy_in.wait()
    copy_out.wait()

    def forward(slot, count):
        span = pl.ds(slot, count)
        gate_up = dot(flat_rows(rbuf[0, span]), w_in[:piece])
        for p in front[1:]:
            gate_up += dot(flat_rows(rbuf[p, span]), w_in[p * piece : (p + 1) * piece])
        gate_part = gate_up[:, :hidden_units]
        up_part = gate_up[:, hidden_units:]
        hidden = gate_part * jax.nn.sigmoid(gate_part) * up_part
        gate_up_buf[span] = gate_up.reshape(count, cap, 2 * hidden_units)
        hid_buf[span] = hidden.reshape(count, cap, hidden_units).astype(BF16)
        hidden = hidden.astype(BF16)
        for p in front:
            value = dot_last(hidden, w_out[p * piece : (p + 1) * piece])
            obuf[p, span] = value.reshape(count, cap, piece).astype(BF16)

    def backward(slot, count):
        span = pl.ds(slot, count)
        hidden_grad = dot(flat_rows(rbuf[cuts, span]), w_out[:piece])
        for q in front[1:]:
            hidden_grad += dot(flat_rows(rbuf[cuts + q, span]), w_out[q * piece : (q + 1) * piece])
        gate_up = gate_up_buf[span].reshape(count * cap, 2 * hidden_units)
        gate_part = gate_up[:, :hidden_units]
        up_part = gate_up[:, hidden_units:]
        sig = jax.nn.sigmoid(gate_part)
        gate_term = hidden_grad * up_part * sig * (1.0 + gate_part * (1.0 - sig))
        up_term = hidden_grad * gate_part * sig
        both = jnp.concatenate([gate_term, up_term], axis=1)
        both_buf[span] = both.reshape(count, cap, 2 * hidden_units).astype(BF16)
        both = both.astype(BF16)
        for q in front:
            value = dot_last(both, w_in[q * piece : (q + 1) * piece])
            obuf[cuts + q, span] = value.reshape(count, cap, piece).astype(BF16)

    def own_pass(work, part):
        work(mine, 1)
        for p in part:
            own_back[p, pl.ds(mine, 1)] = obuf[p, pl.ds(mine, 1)]

        def one(k, carry):
            i = lax.rem(mine + k, h)
            for p in part:
                own_arrival(p, i).wait_recv()
            work(i, 1)
            for p in part:
                own_return(p, i).start()
            return carry

        lax.fori_loop(1, h, one, 0)

    def far_pass(work, part):
        def one(k, carry):
            r = lax.rem(my_relay + k, relays)
            myself = jnp.logical_and(is_relay, r == my_relay)

            @pl.when(jnp.logical_not(myself))
            def _():
                for p in part:
                    far_arrival(p, r).wait_recv()

            work(h + 2 * r, 2)

            @pl.when(myself)
            def _():
                for p in part:
                    far_back[p, mine] = obuf[p, pl.ds(h + 2 * r, 2)]

            @pl.when(jnp.logical_not(myself))
            def _():
                for p in part:
                    far_return(p, r).start()

            return carry

        lax.fori_loop(0, relays, one, 0)

    def relay_out(p):
        @pl.when(is_relay)
        def _():
            for f in range(2):
                if p == 0:
                    info_arrival(f).wait_recv()
                raw_arrival(p, f).wait_recv()
                value = dot(place_rows(info_got[f, :1, :]), raw_got[p, f])
                far_send[p, :, f] = value.reshape(h, cap, piece).astype(BF16)
            for k in range(1, h):
                far_copy(p, lax.rem(mine + k, h)).start()
            rbuf[p, pl.ds(h + 2 * my_relay, 2)] = far_send[p, mine]

    def relay_in(part):
        @pl.when(is_relay)
        def _():
            picks = []
            for f in range(2):
                col = jnp.sum(jnp.where(eye, info_got[f, :1, :], 0.0), axis=1, keepdims=True)
                picks.append(pick_rows(col))
            for p in part:
                for k in range(1, h):
                    far_returned(p, lax.rem(mine + k, h)).wait_recv()
                for f in range(2):
                    relay_send[p, f] = dot(picks[f], flat_rows(far_back[p, :, f])).astype(BF16)
                    relay_copy(p, f).start()

    own_pass(forward, front)
    for p in front:
        relay_out(p)
    own_pass(backward, rear)
    for p in rear[:-1]:
        relay_out(p)
    far_pass(forward, front)
    relay_out(rear[-1])
    relay_in(front)
    far_pass(backward, rear)

    both_all = flat_rows(both_buf[...])
    hid_all = flat_rows(hid_buf[...])
    share = width // n_dp
    blocks = n_dp // cuts
    for q in front:
        into = pl.ds(q * blocks, blocks)
        wacc[into, :, : 2 * hidden_units] = dot_rows(flat_rows(rbuf[q]), both_all).reshape(
            blocks, share, 2 * hidden_units)
        wacc[into, :, 2 * hidden_units :] = dot_rows(flat_rows(rbuf[cuts + q]), hid_all).reshape(
            blocks, share, hidden_units)

    def pair_copy(j):
        return pltpu.make_async_remote_copy(
            src_ref=wsend1.at[j], dst_ref=wrecv1.at[j],
            send_sem=ws1.at[j], recv_sem=wr1.at[j],
            device_id={"dp": other}, device_id_type=MESH)

    for k in range(half):
        j = lax.rem(pair + 1 + k, half)
        wsend1[j] = wacc[2 * j + 1 - core].astype(BF16)
        pair_copy(j).start()

    def group_copy(j):
        return pltpu.make_async_remote_copy(
            src_ref=wsend2.at[j], dst_ref=wrecv2.at[pair],
            send_sem=ws2.at[j], recv_sem=wr2.at[pair],
            device_id={"dp": 2 * j + core}, device_id_type=MESH)

    def group_arrival(j):
        return pltpu.make_async_remote_copy(
            src_ref=wsend2.at[j], dst_ref=wrecv2.at[j],
            send_sem=ws2.at[j], recv_sem=wr2.at[j],
            device_id={"dp": 2 * j + core}, device_id_type=MESH)

    for k in range(1, half):
        j = lax.rem(pair + k, half)
        pair_copy(j).wait_recv()
        wsend2[j] = (wacc[2 * j + core] + wrecv1[j].astype(F32)).astype(BF16)
        group_copy(j).start()

    relay_in(rear)

    picks = pick_rows(slot_col)
    for k in range(1, h):
        for p in every:
            own_returned(p, lax.rem(mine + k, h)).wait_recv()
    sums = jnp.zeros((rows, 1), F32)
    for p in front:
        into = pl.ds(p * piece, piece)
        relayed(p).wait_recv()
        ffn = dot(picks, flat_rows(own_back[p])) + relay_back[p].astype(F32)
        mixed[:, into] = (gate * ffn).astype(BF16)
        sums += jnp.sum(out_grad[:, into].astype(F32) * ffn, axis=1, keepdims=True)
    gate_grad[...] = jnp.sum(jnp.where(eye, sums, 0.0), axis=0, keepdims=True)

    pair_copy(pair).wait_recv()
    total = wacc[dp] + wrecv1[pair].astype(F32)
    for k in range(1, half):
        j = lax.rem(pair + k, half)
        group_arrival(j).wait_recv()
        total = total + wrecv2[j].astype(F32)
    grad_in[0] = total[:, : 2 * hidden_units]
    grad_out[0] = total[:, 2 * hidden_units :]

    for q in front:
        p = cuts + q
        relayed(p).wait_recv()
        value = dot(picks, flat_rows(own_back[p])) + relay_back[p].astype(F32)
        input_rows[:, pl.ds(q * piece, piece)] = value.astype(BF16)

    info_copy().wait_send()
    for p in every:
        raw_copy(p).wait_send()
        for k in range(1, h):
            i = lax.rem(mine + k, h)
            own_copy(p, i).wait_send()
            own_return(p, i).wait_send()
        for r in range(relays):
            @pl.when(jnp.logical_not(jnp.logical_and(is_relay, my_relay == r)))
            def _():
                far_return(p, r).wait_send()

    @pl.when(is_relay)
    def _():
        for p in every:
            for k in range(1, h):
                far_copy(p, lax.rem(mine + k, h)).wait_send()
            for f in range(2):
                relay_copy(p, f).wait_send()
    for j in range(half):
        pair_copy(j).wait_send()
    for k in range(1, half):
        group_copy(lax.rem(pair + k, half)).wait_send()


def pass_on(*refs):
    count = len(refs) // 2
    for source, target in zip(refs[:count], refs[count:]):
        target[...] = source[...]


def on_device(n, n_dp, tokens, expert_ids, gate_scale, w_gate_up, w_down, out_grad):
    rows, width = tokens.shape
    hidden_units = w_down.shape[2]
    cap = 3 * rows // n
    share = width // n_dp
    half = n_dp // 2
    terms = 3 * hidden_units
    cuts = 2
    piece = width // cuts
    both = 2 * cuts
    h = n // 2
    relays = h // 2
    vmem = pl.BlockSpec(memory_space=pltpu.VMEM)
    anywhere = pl.BlockSpec(memory_space=pl.ANY)
    dma = pltpu.SemaphoreType.DMA
    shapes = (
        jax.ShapeDtypeStruct((rows, width), BF16),
        jax.ShapeDtypeStruct((rows, width), BF16),
        jax.ShapeDtypeStruct((1, rows), F32),
        jax.ShapeDtypeStruct((1, share, 2 * hidden_units), F32),
        jax.ShapeDtypeStruct((1, share, hidden_units), F32),
    )
    results = pl.pallas_call(
        functools.partial(kernel, n, n_dp, cap, cuts),
        out_shape=shapes,
        in_specs=[anywhere] * 6,
        out_specs=(vmem,) * 5,
        scratch_shapes=[
            pltpu.VMEM((rows, width), BF16),
            pltpu.VMEM((1, rows), jnp.int32),
            pltpu.VMEM((1, rows), F32),
            pltpu.VMEM((rows, width), BF16),
            pltpu.VMEM((width, 2 * hidden_units), BF16),
            pltpu.VMEM((width, hidden_units), BF16),
            pltpu.VMEM((rows, width), BF16),
            pltpu.VMEM((8, rows), F32),
            pltpu.VMEM((2, 8, rows), F32),
            pltpu.VMEM((both, 2, rows, piece), BF16),
            pltpu.VMEM((both, h, cap, piece), BF16),
            pltpu.VMEM((both, h, 2, cap, piece), BF16),
            pltpu.VMEM((both, n, cap, piece), BF16),
            pltpu.VMEM((both, n, cap, piece), BF16),
            pltpu.VMEM((both, h, cap, piece), BF16),
            pltpu.VMEM((both, h, 2, cap, piece), BF16),
            pltpu.VMEM((both, 2, rows, piece), BF16),
            pltpu.VMEM((both, rows, piece), BF16),
            pltpu.VMEM((n, cap, 2 * hidden_units), F32),
            pltpu.VMEM((n, cap, 2 * hidden_units), BF16),
            pltpu.VMEM((n, cap, hidden_units), BF16),
            pltpu.VMEM((n_dp, share, terms), F32),
            pltpu.VMEM((half, share, terms), BF16),
            pltpu.VMEM((half, share, terms), BF16),
            pltpu.VMEM((half, share, terms), BF16),
            pltpu.VMEM((half, share, terms), BF16),
            dma((6,)), dma((1,)), dma((2,)),
            dma((both,)), dma((both, 2)),
            dma((both, h)), dma((both, h)),
            dma((both, h)), dma((both, relays)),
            dma((both, h)), dma((both, h)),
            dma((both, relays)), dma((both, h)),
            dma((both, 2)), dma((both,)),
            dma((half,)), dma((half,)), dma((half,)), dma((half,)),
        ],
        compiler_params=pltpu.CompilerParams(
            collective_id=0, has_side_effects=True, vmem_limit_bytes=63 * 1024 * 1024),
    )(tokens, expert_ids.reshape(1, rows), gate_scale[None, :], w_gate_up, w_down, out_grad)
    mixed, input_rows, gate_grad, grad_in, grad_out = pl.pallas_call(
        pass_on,
        out_shape=shapes,
        in_specs=[vmem] * 5,
        out_specs=(vmem,) * 5,
    )(*results)
    return mixed, input_rows, gate_grad[0], grad_in, grad_out


def solution(mesh):
    return jax.shard_map(
        functools.partial(on_device, mesh.shape["expert"], mesh.shape["dp"]),
        mesh=mesh,
        in_specs=(
            P(("dp", "expert"), None),
            P(("dp", "expert"), None),
            P(("dp", "expert")),
            P("expert", None, None),
            P("expert", None, None),
            P(("dp", "expert"), None),
        ),
        out_specs=(
            P(("dp", "expert"), None),
            P(("dp", "expert"), None),
            P(("dp", "expert")),
            P("expert", "dp", None),
            P("expert", "dp", None),
        ),
        check_vma=False,
    )
```

```python
import functools

import jax
import jax.numpy as jnp
from jax import lax
from jax.experimental import pallas as pl
from jax.experimental.pallas import tpu as pltpu
from jax.sharding import PartitionSpec as P

F32 = jnp.float32
BF16 = jnp.bfloat16
MESH = pl.DeviceIdType.MESH


def dot(left, right):
    return jnp.dot(left, right, preferred_element_type=F32)


def dot_last(left, right):
    return lax.dot_general(left, right, (((1,), (1,)), ((), ())), preferred_element_type=F32)


def dot_rows(left, right):
    return lax.dot_general(left, right, (((0,), (0,)), ((), ())), preferred_element_type=F32)


def flat_rows(value):
    lead, cap, width = value.shape
    if cap % 16:
        return value.astype(F32).reshape(lead * cap, width).astype(BF16)
    return value.reshape(lead * cap, width)


def kernel(
    n, n_dp, cap, cuts,
    tokens_hbm, ids_hbm, gate_hbm, w_in_hbm, w_out_hbm, grad_hbm,
    mixed, input_rows, gate_grad, grad_in, grad_out,
    tokens, ids_row, gate_row, out_grad, w_in, w_out, scaled_buf, info, info_got, raw_got, own_send, far_send, rbuf, obuf,
    own_back, far_back, relay_send, relay_back, gate_up_buf, both_buf, hid_buf,
    wacc, wsend1, wrecv1, wsend2, wrecv2,
    w_sem, is_sem, ir_sem, raw_s, raw_r, own_s, own_r, far_s, far_r,
    ob_s, ob_r, fb_s, fb_r, rb_s, rb_r, ws1, wr1, ws2, wr2,
):
    rows, width = tokens.shape
    hidden_units = w_out.shape[1]
    piece = width // cuts
    h = n // 2
    relays = h // 2
    me = lax.axis_index("expert")
    dp = lax.axis_index("dp")
    half = n_dp // 2
    core = lax.rem(dp, 2)
    pair = lax.div(dp, 2)
    other = dp + 1 - 2 * core
    upper = lax.div(me, h)
    base = upper * h
    mine = me - base
    my_relay = lax.rem(mine, relays)
    my_lane = lax.div(mine, relays)
    relay_start = base + (1 - upper) * relays
    far_relay = (1 - upper) * h + upper * relays + my_relay
    is_relay = lax.div(mine, relays) == 1 - upper
    far_base = (1 - upper) * h

    def remote(source, target, send, receive, peer):
        return pltpu.make_async_remote_copy(
            src_ref=source, dst_ref=target, send_sem=send, recv_sem=receive,
            device_id={"expert": peer}, device_id_type=MESH)

    copy_in = pltpu.make_async_copy(w_in_hbm.at[0], w_in, w_sem.at[0])
    copy_out = pltpu.make_async_copy(w_out_hbm.at[0], w_out, w_sem.at[1])
    loads = [
        pltpu.make_async_copy(source, target, w_sem.at[2 + i])
        for i, (source, target) in enumerate((
            (ids_hbm, ids_row), (gate_hbm, gate_row), (tokens_hbm, tokens), (grad_hbm, out_grad)))
    ]
    for load in loads:
        load.start()
    copy_in.start()
    copy_out.start()

    barrier = pltpu.get_barrier_semaphore()
    for k in range(1, n):
        pl.semaphore_signal(barrier, inc=1, device_id={"expert": lax.rem(me + k, n)}, device_id_type=MESH)
    pl.semaphore_signal(barrier, inc=1, device_id={"dp": other}, device_id_type=MESH)
    for j in range(1, half):
        pl.semaphore_signal(barrier, inc=1, device_id={"dp": lax.rem(dp + 2 * j, n_dp)}, device_id_type=MESH)

    for load in loads:
        load.wait()
    lane = lax.broadcasted_iota(jnp.int32, (rows, rows), 1)
    line = lax.broadcasted_iota(jnp.int32, (rows, rows), 0)
    eye = lane == line
    ids_f = ids_row[...].astype(F32)
    ids_col = jnp.sum(jnp.where(eye, ids_f, 0.0), axis=1, keepdims=True)
    onehot = jnp.where(lane.astype(F32) == ids_col, 1.0, 0.0)
    lower = jnp.where(lane < line, 1.0, 0.0).astype(BF16)
    before = dot(lower, onehot.astype(BF16))
    position = jnp.sum(before * onehot, axis=1, keepdims=True)
    slot_col = ids_col * float(cap) + position
    slot_row = jnp.sum(jnp.where(eye, slot_col, 0.0), axis=0, keepdims=True)
    info[...] = jnp.broadcast_to(slot_row, info.shape)
    gate = jnp.sum(jnp.where(eye, gate_row[...], 0.0), axis=1, keepdims=True)
    scaled_buf[...] = (gate * out_grad[...].astype(F32)).astype(BF16)

    def place_rows(row):
        spot = lax.broadcasted_iota(jnp.int32, (h * cap, rows), 0) + base * cap
        return jnp.where(spot == row.astype(jnp.int32), 1.0, 0.0).astype(BF16)

    def pick_rows(col):
        spot = lax.broadcasted_iota(jnp.int32, (rows, h * cap), 1) + base * cap
        return jnp.where(spot == col.astype(jnp.int32), 1.0, 0.0).astype(BF16)

    def columns(ref, p):
        q = p % cuts
        return ref.at[:, pl.ds(q * piece, piece)]

    def raw_source(p):
        return columns(tokens if p < cuts else scaled_buf, p)

    def raw_copy(p):
        return remote(raw_source(p), raw_got.at[p, my_lane], raw_s.at[p], raw_r.at[p, my_lane], far_relay)

    def raw_arrival(p, f):
        return remote(raw_source(p), raw_got.at[p, f], raw_s.at[p], raw_r.at[p, f], far_relay)

    def own_copy(p, i):
        return remote(own_send.at[p, i], rbuf.at[p, mine], own_s.at[p, i], own_r.at[p, mine], base + i)

    def own_arrival(p, i):
        return remote(own_send.at[p, i], rbuf.at[p, i], own_s.at[p, i], own_r.at[p, i], base + i)

    def far_copy(p, i):
        return remote(far_send.at[p, i], rbuf.at[p, pl.ds(h + 2 * my_relay, 2)],
                      far_s.at[p, i], far_r.at[p, my_relay], base + i)

    def far_arrival(p, r):
        return remote(far_send.at[p, 0], rbuf.at[p, pl.ds(h + 2 * r, 2)],
                      far_s.at[p, 0], far_r.at[p, r], relay_start + r)

    def own_return(p, i):
        return remote(obuf.at[p, i], own_back.at[p, mine], ob_s.at[p, i], ob_r.at[p, mine], base + i)

    def own_returned(p, i):
        return remote(obuf.at[p, i], own_back.at[p, i], ob_s.at[p, i], ob_r.at[p, i], base + i)

    def far_return(p, r):
        return remote(obuf.at[p, pl.ds(h + 2 * r, 2)], far_back.at[p, mine],
                      fb_s.at[p, r], fb_r.at[p, mine], relay_start + r)

    def far_returned(p, i):
        return remote(obuf.at[p, pl.ds(h, 2)], far_back.at[p, i], fb_s.at[p, 0], fb_r.at[p, i], base + i)

    def relay_copy(p, f):
        return remote(relay_send.at[p, f], relay_back.at[p], rb_s.at[p, f], rb_r.at[p],
                      far_base + f * relays + my_relay)

    def relayed(p):
        return remote(relay_send.at[p, 0], relay_back.at[p], rb_s.at[p, 0], rb_r.at[p], far_relay)

    def info_copy():
        return remote(info, info_got.at[my_lane], is_sem.at[0], ir_sem.at[my_lane], far_relay)

    def info_arrival(f):
        return remote(info, info_got.at[f], is_sem.at[0], ir_sem.at[f], far_relay)

    front, rear = range(cuts), range(cuts, 2 * cuts)
    every = range(2 * cuts)
    own_places = place_rows(slot_row)
    pl.semaphore_wait(barrier, n - 1 + half)
    info_copy().start()
    for p in every:
        raw_copy(p).start()
        own_send[p] = dot(own_places, raw_source(p)[...]).reshape(h, cap, piece).astype(BF16)
        for k in range(1, h):
            own_copy(p, lax.rem(mine + k, h)).start()
        rbuf[p, pl.ds(mine, 1)] = own_send[p, pl.ds(mine, 1)]

    copy_in.wait()
    copy_out.wait()

    def forward(slot, count):
        span = pl.ds(slot, count)
        gate_up = dot(flat_rows(rbuf[0, span]), w_in[:piece])
        for p in front[1:]:
            gate_up += dot(flat_rows(rbuf[p, span]), w_in[p * piece : (p + 1) * piece])
        gate_part = gate_up[:, :hidden_units]
        up_part = gate_up[:, hidden_units:]
        hidden = gate_part * jax.nn.sigmoid(gate_part) * up_part
        gate_up_buf[span] = gate_up.reshape(count, cap, 2 * hidden_units)
        hid_buf[span] = hidden.reshape(count, cap, hidden_units).astype(BF16)
        hidden = hidden.astype(BF16)
        for p in front:
            value = dot_last(hidden, w_out[p * piece : (p + 1) * piece])
            obuf[p, span] = value.reshape(count, cap, piece).astype(BF16)

    def backward(slot, count):
        span = pl.ds(slot, count)
        hidden_grad = dot(flat_rows(rbuf[cuts, span]), w_out[:piece])
        for q in front[1:]:
            hidden_grad += dot(flat_rows(rbuf[cuts + q, span]), w_out[q * piece : (q + 1) * piece])
        gate_up = gate_up_buf[span].reshape(count * cap, 2 * hidden_units)
        gate_part = gate_up[:, :hidden_units]
        up_part = gate_up[:, hidden_units:]
        sig = jax.nn.sigmoid(gate_part)
        gate_term = hidden_grad * up_part * sig * (1.0 + gate_part * (1.0 - sig))
        up_term = hidden_grad * gate_part * sig
        both = jnp.concatenate([gate_term, up_term], axis=1)
        both_buf[span] = both.reshape(count, cap, 2 * hidden_units).astype(BF16)
        both = both.astype(BF16)
        for q in front:
            value = dot_last(both, w_in[q * piece : (q + 1) * piece])
            obuf[cuts + q, span] = value.reshape(count, cap, piece).astype(BF16)

    def own_pass(work, part):
        work(mine, 1)
        for p in part:
            own_back[p, pl.ds(mine, 1)] = obuf[p, pl.ds(mine, 1)]

        def one(k, carry):
            i = lax.rem(mine + k, h)
            for p in part:
                own_arrival(p, i).wait_recv()
            work(i, 1)
            for p in part:
                own_return(p, i).start()
            return carry

        lax.fori_loop(1, h, one, 0)

    def far_pass(work, part):
        def one(k, carry):
            r = lax.rem(my_relay + k, relays)
            myself = jnp.logical_and(is_relay, r == my_relay)

            @pl.when(jnp.logical_not(myself))
            def _():
                for p in part:
                    far_arrival(p, r).wait_recv()

            work(h + 2 * r, 2)

            @pl.when(myself)
            def _():
                for p in part:
                    far_back[p, mine] = obuf[p, pl.ds(h + 2 * r, 2)]

            @pl.when(jnp.logical_not(myself))
            def _():
                for p in part:
                    far_return(p, r).start()

            return carry

        lax.fori_loop(0, relays, one, 0)

    def relay_out(p):
        @pl.when(is_relay)
        def _():
            for f in range(2):
                if p == 0:
                    info_arrival(f).wait_recv()
                raw_arrival(p, f).wait_recv()
                value = dot(place_rows(info_got[f, :1, :]), raw_got[p, f])
                far_send[p, :, f] = value.reshape(h, cap, piece).astype(BF16)
            for k in range(1, h):
                far_copy(p, lax.rem(mine + k, h)).start()
            rbuf[p, pl.ds(h + 2 * my_relay, 2)] = far_send[p, mine]

    def relay_in(part):
        @pl.when(is_relay)
        def _():
            picks = []
            for f in range(2):
                col = jnp.sum(jnp.where(eye, info_got[f, :1, :], 0.0), axis=1, keepdims=True)
                picks.append(pick_rows(col))
            for p in part:
                for k in range(1, h):
                    far_returned(p, lax.rem(mine + k, h)).wait_recv()
                for f in range(2):
                    relay_send[p, f] = dot(picks[f], flat_rows(far_back[p, :, f])).astype(BF16)
                    relay_copy(p, f).start()

    relay_out(0)
    own_pass(forward, front)
    for p in front[1:]:
        relay_out(p)
    for p in rear[:-1]:
        relay_out(p)
    far_pass(forward, front)
    relay_out(rear[-1])
    own_pass(backward, rear)
    relay_in(front)
    far_pass(backward, rear)

    both_all = flat_rows(both_buf[...])
    hid_all = flat_rows(hid_buf[...])
    share = width // n_dp
    blocks = n_dp // cuts
    for q in front:
        into = pl.ds(q * blocks, blocks)
        wacc[into, :, : 2 * hidden_units] = dot_rows(flat_rows(rbuf[q]), both_all).reshape(
            blocks, share, 2 * hidden_units)
        wacc[into, :, 2 * hidden_units :] = dot_rows(flat_rows(rbuf[cuts + q]), hid_all).reshape(
            blocks, share, hidden_units)

    def pair_copy(j):
        return pltpu.make_async_remote_copy(
            src_ref=wsend1.at[j], dst_ref=wrecv1.at[j],
            send_sem=ws1.at[j], recv_sem=wr1.at[j],
            device_id={"dp": other}, device_id_type=MESH)

    for k in range(half):
        j = lax.rem(pair + 1 + k, half)
        wsend1[j] = wacc[2 * j + 1 - core].astype(BF16)
        pair_copy(j).start()

    def group_copy(j):
        return pltpu.make_async_remote_copy(
            src_ref=wsend2.at[j], dst_ref=wrecv2.at[pair],
            send_sem=ws2.at[j], recv_sem=wr2.at[pair],
            device_id={"dp": 2 * j + core}, device_id_type=MESH)

    def group_arrival(j):
        return pltpu.make_async_remote_copy(
            src_ref=wsend2.at[j], dst_ref=wrecv2.at[j],
            send_sem=ws2.at[j], recv_sem=wr2.at[j],
            device_id={"dp": 2 * j + core}, device_id_type=MESH)

    for k in range(1, half):
        j = lax.rem(pair + k, half)
        pair_copy(j).wait_recv()
        wsend2[j] = (wacc[2 * j + core] + wrecv1[j].astype(F32)).astype(BF16)
        group_copy(j).start()

    relay_in(rear)

    picks = pick_rows(slot_col)
    for k in range(1, h):
        for p in every:
            own_returned(p, lax.rem(mine + k, h)).wait_recv()
    sums = jnp.zeros((rows, 1), F32)
    for p in front:
        into = pl.ds(p * piece, piece)
        relayed(p).wait_recv()
        ffn = dot(picks, flat_rows(own_back[p])) + relay_back[p].astype(F32)
        mixed[:, into] = (gate * ffn).astype(BF16)
        sums += jnp.sum(out_grad[:, into].astype(F32) * ffn, axis=1, keepdims=True)
    gate_grad[...] = jnp.sum(jnp.where(eye, sums, 0.0), axis=0, keepdims=True)

    pair_copy(pair).wait_recv()
    total = wacc[dp] + wrecv1[pair].astype(F32)
    for k in range(1, half):
        j = lax.rem(pair + k, half)
        group_arrival(j).wait_recv()
        total = total + wrecv2[j].astype(F32)
    grad_in[0] = total[:, : 2 * hidden_units]
    grad_out[0] = total[:, 2 * hidden_units :]

    for q in front:
        p = cuts + q
        relayed(p).wait_recv()
        value = dot(picks, flat_rows(own_back[p])) + relay_back[p].astype(F32)
        input_rows[:, pl.ds(q * piece, piece)] = value.astype(BF16)

    info_copy().wait_send()
    for p in every:
        raw_copy(p).wait_send()
        for k in range(1, h):
            i = lax.rem(mine + k, h)
            own_copy(p, i).wait_send()
            own_return(p, i).wait_send()
        for r in range(relays):
            @pl.when(jnp.logical_not(jnp.logical_and(is_relay, my_relay == r)))
            def _():
                far_return(p, r).wait_send()

    @pl.when(is_relay)
    def _():
        for p in every:
            for k in range(1, h):
                far_copy(p, lax.rem(mine + k, h)).wait_send()
            for f in range(2):
                relay_copy(p, f).wait_send()
    for j in range(half):
        pair_copy(j).wait_send()
    for k in range(1, half):
        group_copy(lax.rem(pair + k, half)).wait_send()


def pass_on(*refs):
    count = len(refs) // 2
    for source, target in zip(refs[:count], refs[count:]):
        target[...] = source[...]


def on_device(n, n_dp, tokens, expert_ids, gate_scale, w_gate_up, w_down, out_grad):
    rows, width = tokens.shape
    hidden_units = w_down.shape[2]
    cap = 3 * rows // n
    share = width // n_dp
    half = n_dp // 2
    terms = 3 * hidden_units
    cuts = 2
    piece = width // cuts
    both = 2 * cuts
    h = n // 2
    relays = h // 2
    vmem = pl.BlockSpec(memory_space=pltpu.VMEM)
    anywhere = pl.BlockSpec(memory_space=pl.ANY)
    dma = pltpu.SemaphoreType.DMA
    shapes = (
        jax.ShapeDtypeStruct((rows, width), BF16),
        jax.ShapeDtypeStruct((rows, width), BF16),
        jax.ShapeDtypeStruct((1, rows), F32),
        jax.ShapeDtypeStruct((1, share, 2 * hidden_units), F32),
        jax.ShapeDtypeStruct((1, share, hidden_units), F32),
    )
    results = pl.pallas_call(
        functools.partial(kernel, n, n_dp, cap, cuts),
        out_shape=shapes,
        in_specs=[anywhere] * 6,
        out_specs=(vmem,) * 5,
        scratch_shapes=[
            pltpu.VMEM((rows, width), BF16),
            pltpu.VMEM((1, rows), jnp.int32),
            pltpu.VMEM((1, rows), F32),
            pltpu.VMEM((rows, width), BF16),
            pltpu.VMEM((width, 2 * hidden_units), BF16),
            pltpu.VMEM((width, hidden_units), BF16),
            pltpu.VMEM((rows, width), BF16),
            pltpu.VMEM((8, rows), F32),
            pltpu.VMEM((2, 8, rows), F32),
            pltpu.VMEM((both, 2, rows, piece), BF16),
            pltpu.VMEM((both, h, cap, piece), BF16),
            pltpu.VMEM((both, h, 2, cap, piece), BF16),
            pltpu.VMEM((both, n, cap, piece), BF16),
            pltpu.VMEM((both, n, cap, piece), BF16),
            pltpu.VMEM((both, h, cap, piece), BF16),
            pltpu.VMEM((both, h, 2, cap, piece), BF16),
            pltpu.VMEM((both, 2, rows, piece), BF16),
            pltpu.VMEM((both, rows, piece), BF16),
            pltpu.VMEM((n, cap, 2 * hidden_units), F32),
            pltpu.VMEM((n, cap, 2 * hidden_units), BF16),
            pltpu.VMEM((n, cap, hidden_units), BF16),
            pltpu.VMEM((n_dp, share, terms), F32),
            pltpu.VMEM((half, share, terms), BF16),
            pltpu.VMEM((half, share, terms), BF16),
            pltpu.VMEM((half, share, terms), BF16),
            pltpu.VMEM((half, share, terms), BF16),
            dma((6,)), dma((1,)), dma((2,)),
            dma((both,)), dma((both, 2)),
            dma((both, h)), dma((both, h)),
            dma((both, h)), dma((both, relays)),
            dma((both, h)), dma((both, h)),
            dma((both, relays)), dma((both, h)),
            dma((both, 2)), dma((both,)),
            dma((half,)), dma((half,)), dma((half,)), dma((half,)),
        ],
        compiler_params=pltpu.CompilerParams(
            collective_id=0, has_side_effects=True, vmem_limit_bytes=63 * 1024 * 1024),
    )(tokens, expert_ids.reshape(1, rows), gate_scale[None, :], w_gate_up, w_down, out_grad)
    mixed, input_rows, gate_grad, grad_in, grad_out = pl.pallas_call(
        pass_on,
        out_shape=shapes,
        in_specs=[vmem] * 5,
        out_specs=(vmem,) * 5,
    )(*results)
    return mixed, input_rows, gate_grad[0], grad_in, grad_out


def solution(mesh):
    return jax.shard_map(
        functools.partial(on_device, mesh.shape["expert"], mesh.shape["dp"]),
        mesh=mesh,
        in_specs=(
            P(("dp", "expert"), None),
            P(("dp", "expert"), None),
            P(("dp", "expert")),
            P("expert", None, None),
            P("expert", None, None),
            P(("dp", "expert"), None),
        ),
        out_specs=(
            P(("dp", "expert"), None),
            P(("dp", "expert"), None),
            P(("dp", "expert")),
            P("expert", "dp", None),
            P("expert", "dp", None),
        ),
        check_vma=False,
    )
```
